32 devices in a mesh: groups: 2 (over y), expert: 4 (over z), mp: 4 (over x, core).
Axes of the slice: x: 2, y: 2, z: 4, core: 2. Of those that a mesh axis runs over, the one named last changes fastest.
Arguments:
- tokens_in: bfloat16 [2048, 2048], P(('groups', 'expert'), 'mp'), parts along dimension 0, may hold values from -6 to 6
- out_grad: bfloat16 [2048, 2048], P(('groups', 'expert'), 'mp'), parts along dimension 0, may hold values from -3 to 3
- logits: float32 [2048, 4], P(('groups', 'expert')), parts along dimension 0, may hold values from -6 to 6
- indices: int32 [8, 256], P('groups'), parts along dimension 0, may hold values from 0 to 1023, as said below
- w_in: bfloat16 [4, 2048, 4096], P('expert', None, 'mp'), may hold values from -0.125 to 0.125
- w_out: bfloat16 [4, 4096, 2048], P('expert', 'mp'), may hold values from -0.09375 to 0.09375
- router_w: bfloat16 [2048, 4], P('mp'), may hold values from -0.125 to 0.125
Outputs:
- input_grad: float32 [2048, 2048], P(('groups', 'expert'), 'mp'), parts along dimension 0
- router_grad: float32 [4096, 4], P(('groups', 'mp')), parts along dimension 0
The draws below stay inside these ranges and needn't reach their ends.
There are 2 independent parts, one for each index of `groups`. The reference program is written for one: setup_inputs(seed, part) draws one part's arguments, and reference() takes and returns one part's arrays. A program takes and returns all parts, laid end to end along the dimension named above; an argument that names none is the same for every part. Nothing has to cross between parts.
Inputs may be any that keep to these rules, and one draw needn't show every extreme that they name: `indices`: each expert's row holds 256 different tokens. Of the 256 tokens of one index of the expert axis (rows k * 256 to (k + 1) * 256 - 1), one expert takes at most 128, and every expert takes exactly 128 from some such index.
All inputs are finite; a program needn't handle non-finite values.
Results may differ from the reference program's by a relative error of at most 0.019.
Values may be sent and summed in bfloat16 or wider, within the bound.
A program may use at most 64 MiB of HBM per device.

```python
import jax
import jax.numpy as jnp
from jax import lax

D = 2048
HIDDEN_SIZE = 4096
CAPACITY = 256
TOK_DEV = 256
EXPERTS = 4
TOKENS = 1024
MOST = 128


def draw_indices(key, part):
    base = jax.random.fold_in(key, 11)
    source_weight = jax.random.randint(jax.random.fold_in(base, 1), (EXPERTS,), 1, 5)
    copies = EXPERTS * MOST
    owner = jnp.arange(copies, dtype=jnp.int32) // MOST
    within = jnp.arange(copies, dtype=jnp.int32) % MOST

    def one_expert(expert_key):
        keys = jax.random.split(expert_key, 3)
        favoured = jax.random.randint(keys[0], (), 0, EXPERTS)
        score = jax.random.randint(keys[1], (copies,), 0, 1024) * source_weight[owner]
        score = score + 8192 * (owner == favoured).astype(jnp.int32)
        score = score * copies + jnp.arange(copies, dtype=jnp.int32)
        unused, picked = lax.top_k(score, CAPACITY)
        shuffle = jax.random.randint(keys[2], (EXPERTS, TOK_DEV), 0, 1 << 20) * TOK_DEV
        shuffle = shuffle + jnp.arange(TOK_DEV, dtype=jnp.int32)[None, :]
        order = jnp.argsort(shuffle, axis=1).astype(jnp.int32)
        picked_owner = owner[picked]
        picked_within = within[picked]
        return picked_owner * TOK_DEV + order[picked_owner, picked_within]
    return jax.vmap(one_expert)(jax.random.split(base, EXPERTS)).astype(jnp.int32)


def steps_of(rng, dims, pieces, least, high):
    gain, own = 1.0, jax.random.fold_in(rng, 6)
    for dim, parts in pieces:
        draws = jnp.exp(jax.random.uniform(jax.random.fold_in(own, dim), (parts,), jnp.float32, least / len(pieces), high / len(pieces)))
        gain = gain * jnp.repeat(draws, dims[dim] // parts).reshape([-1 if axis == dim else 1 for axis in range(len(dims))])
    return gain


def bell_draw(rng, dims, deviation, most, cuts=(), kind=jnp.bfloat16):
    array = deviation * jax.random.normal(rng, dims, jnp.float32)
    if cuts:
        array = array * steps_of(rng, dims, cuts, -0.22, 0.18)
    return jnp.clip(array, -most, most).astype(kind)


def setup_inputs(seed: int = 0, part: int = 0) -> dict:
    key_of = jax.random.split(jax.random.key(seed), 8)
    part_splits = jax.random.split(jax.random.fold_in(key_of[7], part), 8)
    tokens_in = bell_draw(part_splits[0], (TOKENS, D), 1.0, 6.0, ((0, 4), (1, 4)))
    out_grad = bell_draw(part_splits[1], (TOKENS, D), 0.5, 3.0, ((0, 4), (1, 4)))
    logits = bell_draw(part_splits[2], (TOKENS, EXPERTS), 1.5, 6.0, ((0, 4),), jnp.float32)
    indices = draw_indices(jax.random.fold_in(jax.random.fold_in(key_of[7], part), 71), part)
    w_in = bell_draw(key_of[4], (EXPERTS, D, HIDDEN_SIZE), D ** -0.5, 0.125, ((0, 4), (2, 4)))
    w_out = bell_draw(key_of[5], (EXPERTS, HIDDEN_SIZE, D), HIDDEN_SIZE ** -0.5, 0.09375, ((0, 4), (1, 4)))
    router_w = bell_draw(key_of[6], (D, EXPERTS), D ** -0.5, 0.125, ((0, 4),))
    return {"tokens_in": tokens_in, "out_grad": out_grad, "logits": logits, "indices": indices, "w_in": w_in, "w_out": w_out, "router_w": router_w}


inv_root_two = 0.7071067811865476
inv_root_tau = 0.3989422804014327


def gelu_parts(hidden_pre):
    cumulative = 0.5 * (1.0 + lax.erf(hidden_pre * inv_root_two))
    slopes = cumulative + hidden_pre * jnp.exp(-0.5 * hidden_pre * hidden_pre) * inv_root_tau
    return hidden_pre * cumulative, slopes


def reference(tokens_in, out_grad, logits, indices, w_in, w_out, router_w):
    def expert_step(packed):
        chosen_idx, weight_in, weight_out = packed
        rows_x = tokens_in[chosen_idx]
        rows_dy = out_grad[chosen_idx]
        hidden_pre = jnp.dot(rows_x, weight_in, preferred_element_type=jnp.float32)
        hidden_back = lax.dot_general(rows_dy, weight_out, (((1,), (1,)), ((), ())), preferred_element_type=jnp.float32)
        activated, slopes = gelu_parts(hidden_pre)
        gate_vals = jnp.sum(activated * hidden_back, axis=1)
        delta = (hidden_back * slopes).astype(jnp.bfloat16)
        contrib = lax.dot_general(delta, weight_in, (((1,), (1,)), ((), ())), preferred_element_type=jnp.float32)
        return contrib.astype(jnp.bfloat16), gate_vals

    contribs, gate_vals = lax.map(expert_step, (indices, w_in, w_out))
    gate_probs = jax.nn.sigmoid(logits)
    expert_ids = jnp.broadcast_to(jnp.arange(EXPERTS, dtype=jnp.int32)[:, None], indices.shape)
    chosen_gates = gate_probs[indices, expert_ids]
    weighted = chosen_gates[:, :, None] * contribs.astype(jnp.float32)
    input_grad = jnp.zeros((TOKENS, D), jnp.float32).at[indices.reshape(-1)].add(weighted.reshape(-1, D))
    gate_grad = jnp.zeros((TOKENS, EXPERTS), jnp.float32).at[indices, expert_ids].add(gate_vals)
    logit_grad = (gate_probs * (1.0 - gate_probs) * gate_grad).astype(jnp.bfloat16)
    router_dx = lax.dot_general(logit_grad, router_w, (((1,), (1,)), ((), ())), preferred_element_type=jnp.float32)
    input_grad = input_grad + router_dx
    router_grad = lax.dot_general(tokens_in, logit_grad, (((0,), (0,)), ((), ())), preferred_element_type=jnp.float32)
    return input_grad, router_grad
```

```python
import functools

import jax
import jax.numpy as jnp
from jax import lax
from jax.experimental import pallas as pl
from jax.experimental.pallas import tpu as pltpu
from jax.sharding import PartitionSpec as P

inv_root_two = 0.7071067811865476
inv_root_tau = 0.3989422804014327
bf16, f32 = jnp.bfloat16, jnp.float32
ROWS = ((0,), (0,))
COLS = ((1,), (1,))
PIECES = 2


def mm(a, b, dims=((1,), (0,))):
    return lax.dot_general(a, b, (dims, ((), ())), preferred_element_type=f32)


def layer_kernel(
    experts, mps, most,
    tok, dy, logits, idx, w_in_hbm, w_out_hbm, router_w,
    out, router_out,
    w_in, w_out, pt, cmat, ctmat, zsend, zrecv, full, pre, back, slopes, delta,
    a_send, a_recv, b_send, b_recv, own_sum, back_send, back_recv,
    gmp, gz, rbuf, lgp, rwp,
    w_sem, zs, zr, ags, agf, agr, as_, ar, bs, br, xs, xr, gms, gmr, gzs, gzr, rs, rr,
):
    k = lax.axis_index("expert")
    m = lax.axis_index("mp")
    half = mps // 2
    h, c = lax.div(m, 2), lax.rem(m, 2)
    partner = h * 2 + (1 - c)
    tok_dev, columns = tok.shape
    cap = idx.shape[1]
    width = columns // PIECES
    hidden = w_in.shape[1]

    def z_of(j):
        return lax.rem(k + (j + experts), experts)

    def h_of(j):
        return lax.rem(h + (j + half), half)

    weight_copies = (
        pltpu.make_async_copy(w_in_hbm.at[0], w_in, w_sem.at[0]),
        pltpu.make_async_copy(w_out_hbm.at[0], w_out, w_sem.at[1]),
    )

    def remote(src, dst, send, recv, **where):
        return pltpu.make_async_remote_copy(
            src_ref=src, dst_ref=dst, send_sem=send, recv_sem=recv,
            device_id=where, device_id_type=pl.DeviceIdType.MESH,
        )

    barrier = pltpu.get_barrier_semaphore()
    for j in range(1, experts):
        pl.semaphore_signal(barrier, inc=1, device_id={"expert": z_of(j)}, device_id_type=pl.DeviceIdType.MESH)
    for i in range(1, mps):
        pl.semaphore_signal(barrier, inc=1, device_id={"mp": lax.rem(m + i, mps)}, device_id_type=pl.DeviceIdType.MESH)
    for copy in weight_copies:
        copy.start()

    tok_col = lax.broadcasted_iota(jnp.int32, (tok_dev, cap), 0) + k * tok_dev
    ones = jnp.ones((cap, most), bf16)
    lower = (
        lax.broadcasted_iota(jnp.int32, (tok_dev, tok_dev), 1)
        < lax.broadcasted_iota(jnp.int32, (tok_dev, tok_dev), 0)
    ).astype(f32).astype(bf16)
    rank_lane = lax.broadcasted_iota(jnp.int32, (tok_dev, most), 1).astype(f32)
    for e in range(experts):
        hit = (idx[e : e + 1, :] == tok_col).astype(f32).astype(bf16)
        mark = mm(hit, ones)
        rank = mm(lower, mark.astype(bf16))
        pt[e] = jnp.where((rank == rank_lane) & (mark > 0.5), 1.0, 0.0).astype(bf16)

    def z_copy(p, j):
        return remote(zsend.at[p, j], zrecv.at[p, j], zs.at[p, j], zr.at[p, j], expert=z_of(j))

    pl.semaphore_wait(barrier, experts - 1 + mps - 1)
    far_first = sorted(range(1, experts), key=lambda j: -min(j, experts - j))
    for p in range(2 * PIECES):
        ref = tok if p < PIECES else dy
        lo = (p % PIECES) * width
        for j in far_first + [0]:
            zsend[p, j] = mm(pt[z_of(j)], ref[:, lo : lo + width], ROWS).astype(bf16)
            if j:
                z_copy(p, j).start()

    mine = idx[pl.ds(k, 1), :]
    slot_c = lax.broadcasted_iota(jnp.int32, (cap, most), 0).astype(f32)
    row_c = lax.broadcasted_iota(jnp.int32, (cap, most), 1).astype(f32)
    slot_t = lax.broadcasted_iota(jnp.int32, (most, cap), 1).astype(f32)
    row_t = lax.broadcasted_iota(jnp.int32, (most, cap), 0).astype(f32)

    def below(row, bound):
        return jnp.sum((row < bound).astype(f32), axis=1, keepdims=True)

    for s in range(experts):
        first = below(mine, s * tok_dev)
        count = below(mine, (s + 1) * tok_dev) - first
        cmat[s] = jnp.where((slot_c - row_c == first) & (row_c < count), 1.0, 0.0).astype(bf16)
        ctmat[s] = jnp.where((slot_t - row_t == first) & (row_t < count), 1.0, 0.0).astype(bf16)

    def ag_slot(j, other):
        return h_of(-j) * 2 + ((1 - c) if other else c)

    def ag_across(p, j):
        return remote(full.at[p, 0], full.at[p, 2 * j], ags.at[p, j], agr.at[p, 2 * j], mp=h_of(j) * 2 + c)

    def ag_pair(p, j):
        return remote(full.at[p, 2 * j], full.at[p, 2 * j + 1], agf.at[p, j], agr.at[p, 2 * j + 1], mp=partner)

    def multiply(p, j, other, first):
        lo = pl.multiple_of(ag_slot(j, other) * columns + (p % PIECES) * width, width)
        rows = full[p, 2 * j + other]
        if p < PIECES:
            term = mm(rows, w_in[pl.ds(lo, width), :])
            acc = pre
        else:
            term = mm(rows, w_out[:, pl.ds(lo, width)], COLS)
            acc = back
        if first:
            acc[...] = term
        else:
            acc[...] += term

    step = 32

    def gelu_rows(i, carry):
        at = pl.ds(pl.multiple_of(i * step, step), step)
        v = pre[at, :]
        cumulative = 0.5 * (1.0 + lax.erf(v * inv_root_two))
        slopes[at, :] = cumulative + v * jnp.exp(-0.5 * v * v) * inv_root_tau
        pre[at, :] = v * cumulative
        return carry

    for p in range(2 * PIECES):
        total = mm(cmat[k], zsend[p, 0])
        for j in sorted(range(1, experts), key=lambda j: min(j, experts - j)):
            z_copy(p, j).wait_recv()
            total += mm(cmat[z_of(-j)], zrecv[p, j])
        full[p, 0] = total.astype(bf16)
        for j in range(1, half):
            ag_across(p, j).start()
        ag_pair(p, 0).start()
        if p == 0:
            weight_copies[0].wait()
        if p == PIECES:
            weight_copies[1].wait()
            lax.fori_loop(0, cap // step, gelu_rows, 0)
        multiply(p, 0, 0, p % PIECES == 0)
        ag_pair(p, 0).wait_recv()
        multiply(p, 0, 1, False)
        for j in range(1, half):
            ag_across(p, j).wait_recv()
            ag_pair(p, j).start()
            multiply(p, j, 0, False)
        for j in range(1, half):
            ag_pair(p, j).wait_recv()
            multiply(p, j, 1, False)

    def delta_rows(i, carry):
        at = pl.ds(pl.multiple_of(i * step, step), step)
        g = back[at, :]
        delta[at, :] = (g * slopes[at, :]).astype(bf16)
        pre[at, 0:1] = jnp.sum(pre[at, :] * g, axis=1, keepdims=True)
        return carry

    lax.fori_loop(0, cap // step, delta_rows, 0)

    def g_mp(i):
        return remote(gmp.at[0], gmp.at[i], gms.at[i], gmr.at[i], mp=lax.rem(m + i, mps))

    def g_z(j):
        return remote(gz.at[0], gz.at[j], gzs.at[j], gzr.at[j], expert=z_of(j))

    eye = lax.broadcasted_iota(jnp.int32, (cap, cap), 0) == lax.broadcasted_iota(jnp.int32, (cap, cap), 1)
    gate_row = jnp.sum(jnp.where(eye, pre[:, 0:1], 0.0), axis=0, keepdims=True)
    gmp[0] = jnp.broadcast_to(gate_row, (8, cap))
    for i in range(1, mps):
        g_mp(i).start()

    def contrib(q, j, other):
        lo = (h_of(j) * 2 + ((1 - c) if other else c)) * columns + q * width
        return mm(delta[...], w_in[pl.ds(pl.multiple_of(lo, width), width), :], COLS)

    def pair_sum(q, j):
        return remote(a_send.at[q, j], a_recv.at[q, j], as_.at[q, j], ar.at[q, j], mp=partner)

    def across_sum(q, j):
        return remote(b_send.at[q, j], b_recv.at[q, j], bs.at[q, j], br.at[q, j], mp=h_of(j) * 2 + c)

    order = list(range(1, half)) + [0]
    for q in range(PIECES):
        for j in order:
            a_send[q, j] = contrib(q, j, 1).astype(bf16)
            pair_sum(q, j).start()
        for j in order:
            mine_sum = contrib(q, j, 0)
            pair_sum(q, j).wait_recv()
            mine_sum += a_recv[q, j].astype(f32)
            if j:
                b_send[q, j] = mine_sum.astype(bf16)
                across_sum(q, j).start()
            else:
                own_sum[q] = mine_sum

    gate_total = gmp[0]
    for i in range(1, mps):
        g_mp(i).wait_recv()
        gate_total += gmp[i]
    gz[0] = gate_total
    for j in range(1, experts):
        g_z(j).start()

    def back_copy(q, j):
        return remote(back_send.at[q, j], back_recv.at[q, j], xs.at[q, j], xr.at[q, j], expert=z_of(j))

    def send_back(q):
        total = own_sum[q]
        for j in range(1, half):
            across_sum(q, j).wait_recv()
            total += b_recv[q, j].astype(f32)
        rows = total.astype(bf16)
        for j in far_first + [0]:
            back_send[q, j] = mm(ctmat[z_of(j)], rows).astype(bf16)
            if j:
                back_copy(q, j).start()

    def r_copy(j):
        return remote(rbuf.at[k], rbuf.at[k], rs.at[j], rr.at[j], expert=z_of(j))

    def r_arrival(j):
        return remote(rbuf.at[z_of(-j)], rbuf.at[z_of(-j)], rs.at[j], rr.at[j], expert=z_of(j))

    send_back(0)

    gate_probs = jax.nn.sigmoid(logits[...])
    lane_e = lax.broadcasted_iota(jnp.int32, (tok_dev, experts), 1)
    slot_lane = lax.broadcasted_iota(jnp.int32, (most, cap), 1).astype(f32)
    rank_col = lax.broadcasted_iota(jnp.int32, (most, cap), 0).astype(f32)
    gate_grad = jnp.zeros((tok_dev, experts), f32)
    for j in range(experts):
        e = z_of(-j)
        if j:
            g_z(j).wait_recv()
        row = gz[j, 0:1, :]
        first = below(idx[pl.ds(e, 1), :], k * tok_dev)
        ranked = jnp.sum(jnp.where(slot_lane - rank_col == first, row, 0.0), axis=1, keepdims=True)
        eye_m = lax.broadcasted_iota(jnp.int32, (most, most), 0) == lax.broadcasted_iota(jnp.int32, (most, most), 1)
        ranked_row = jnp.sum(jnp.where(eye_m, ranked, 0.0), axis=0, keepdims=True)
        picked = jnp.sum(jnp.where(pt[e].astype(f32) > 0.5, ranked_row, 0.0), axis=1, keepdims=True)
        gate_grad = jnp.where(lane_e == e, picked, gate_grad)
    logit_grad = (gate_probs * (1.0 - gate_probs) * gate_grad).astype(bf16)
    lgp[...] = jnp.zeros_like(lgp)
    rwp[...] = jnp.zeros_like(rwp)
    lgp[:, 0:experts] = logit_grad
    rwp[:, 0:experts] = router_w[...]
    local = mm(lgp[...], tok[...], ROWS)
    rbuf[k] = local[0 : rbuf.shape[1], :]
    for j in range(1, experts):
        r_copy(j).start()
    out[...] = mm(lgp[...], rwp[...], COLS)

    for q in range(1, PIECES):
        send_back(q)

    for q in range(PIECES):
        lo = q * width
        total = out[:, lo : lo + width]
        for j in [0] + far_first[::-1]:
            e = z_of(-j)
            gate = jnp.sum(jnp.where(lane_e == e, gate_probs, 0.0), axis=1, keepdims=True)
            spread = (pt[e].astype(f32) * gate).astype(bf16)
            if j:
                back_copy(q, j).wait_recv()
                total += mm(spread, back_recv[q, j])
            else:
                total += mm(spread, back_send[q, 0])
        out[:, lo : lo + width] = total

    for j in range(1, experts):
        r_arrival(j).wait_recv()
    summed = rbuf[0]
    for e in range(1, experts):
        summed += rbuf[e]
    router_out[...] = summed

    for p in range(2 * PIECES):
        for j in range(1, experts):
            z_copy(p, j).wait_send()
        for j in range(1, half):
            ag_across(p, j).wait_send()
        for j in range(half):
            ag_pair(p, j).wait_send()
    for i in range(1, mps):
        g_mp(i).wait_send()
    for q in range(PIECES):
        for j in range(half):
            pair_sum(q, j).wait_send()
        for j in range(1, half):
            across_sum(q, j).wait_send()
        for j in range(1, experts):
            back_copy(q, j).wait_send()
    for j in range(1, experts):
        g_z(j).wait_send()
        r_copy(j).wait_send()


def per_device(experts, mps, tokens_in, out_grad, logits, indices, w_in, w_out, router_w):
    tok_dev, columns = tokens_in.shape
    cap = indices.shape[1]
    most = min(tok_dev, 2 * cap // experts)
    width = columns // PIECES
    half = mps // 2
    features, hidden = w_in.shape[1:]
    rows8 = -(-experts // 8) * 8
    lanes = -(-experts // 128) * 128
    vmem = pl.BlockSpec(memory_space=pltpu.VMEM)
    hbm = pl.BlockSpec(memory_space=pl.ANY)
    dma = pltpu.SemaphoreType.DMA
    input_grad, router_rows = pl.pallas_call(
        functools.partial(layer_kernel, experts, mps, most),
        out_shape=(
            jax.ShapeDtypeStruct((tok_dev, columns), f32),
            jax.ShapeDtypeStruct((rows8, columns), f32),
        ),
        in_specs=[vmem, vmem, vmem, vmem, hbm, hbm, vmem],
        out_specs=(vmem, vmem),
        scratch_shapes=[
            pltpu.VMEM((features, hidden), bf16),
            pltpu.VMEM((hidden, features), bf16),
            pltpu.VMEM((experts, tok_dev, most), bf16),
            pltpu.VMEM((experts, cap, most), bf16),
            pltpu.VMEM((experts, most, cap), bf16),
            pltpu.VMEM((2 * PIECES, experts, most, width), bf16),
            pltpu.VMEM((2 * PIECES, experts, most, width), bf16),
            pltpu.VMEM((2 * PIECES, mps, cap, width), bf16),
            pltpu.VMEM((cap, hidden), f32),
            pltpu.VMEM((cap, hidden), f32),
            pltpu.VMEM((cap, hidden), f32),
            pltpu.VMEM((cap, hidden), bf16),
            pltpu.VMEM((PIECES, half, cap, width), bf16),
            pltpu.VMEM((PIECES, half, cap, width), bf16),
            pltpu.VMEM((PIECES, half, cap, width), bf16),
            pltpu.VMEM((PIECES, half, cap, width), bf16),
            pltpu.VMEM((PIECES, cap, width), f32),
            pltpu.VMEM((PIECES, experts, most, width), bf16),
            pltpu.VMEM((PIECES, experts, most, width), bf16),
            pltpu.VMEM((mps, 8, cap), f32),
            pltpu.VMEM((experts, 8, cap), f32),
            pltpu.VMEM((experts, rows8, columns), f32),
            pltpu.VMEM((tok_dev, lanes), bf16),
            pltpu.VMEM((columns, lanes), bf16),
            dma((2,)),
            dma((2 * PIECES, experts)),
            dma((2 * PIECES, experts)),
            dma((2 * PIECES, half)),
            dma((2 * PIECES, half)),
            dma((2 * PIECES, mps)),
            dma((PIECES, half)),
            dma((PIECES, half)),
            dma((PIECES, half)),
            dma((PIECES, half)),
            dma((PIECES, experts)),
            dma((PIECES, experts)),
            dma((mps,)),
            dma((mps,)),
            dma((experts,)),
            dma((experts,)),
            dma((experts,)),
            dma((experts,)),
        ],
        compiler_params=pltpu.CompilerParams(collective_id=0, has_side_effects=True),
    )(tokens_in, out_grad, logits, indices, w_in, w_out, router_w)
    return input_grad, router_rows[:experts].T


def solution(mesh):
    return jax.shard_map(
        functools.partial(per_device, mesh.shape["expert"], mesh.shape["mp"]),
        mesh=mesh,
        in_specs=(
            P(("groups", "expert"), "mp"),
            P(("groups", "expert"), "mp"),
            P(("groups", "expert"), None),
            P("groups", None),
            P("expert", None, "mp"),
            P("expert", "mp", None),
            P("mp", None),
        ),
        out_specs=(P(("groups", "expert"), "mp"), P(("groups", "mp"), None)),
        check_vma=False,
    )
```

```python
import functools

import jax
import jax.numpy as jnp
from jax import lax
from jax.experimental import pallas as pl
from jax.experimental.pallas import tpu as pltpu
from jax.sharding import PartitionSpec as P

inv_root_two = 0.7071067811865476
inv_root_tau = 0.3989422804014327
bf16, f32 = jnp.bfloat16, jnp.float32
ROWS = ((0,), (0,))
COLS = ((1,), (1,))
CHUNKS = 2
PIECES = 1


def mm(a, b, dims=((1,), (0,))):
    return lax.dot_general(a, b, (dims, ((), ())), preferred_element_type=f32)


def layer_kernel(
    experts, mps, chunks, pieces,
    tok, dy, logits, idx, w_in_hbm, w_out_hbm, router_w,
    out, router_out,
    w_in, w_out, pt, spread, cmat, ctmat, zsend, zrecv, full, pre, back, slopes, delta,
    a_send, a_recv, b_send, b_recv, own_sum, back_send, back_recv,
    gmp, gz, rbuf, lgp, rwp,
    w_sem, zs, zr, ags, agf, agr, as_, ar, bs, br, xs, xr, gms, gmr, gzs, gzr, rs, rr,
):
    k = lax.axis_index("expert")
    m = lax.axis_index("mp")
    half = mps // 2
    h, c = lax.div(m, 2), lax.rem(m, 2)
    partner = h * 2 + (1 - c)
    tok_dev, columns = tok.shape
    slots = pre.shape[1]
    most = pt.shape[3]
    width = columns // pieces
    started = []

    def z_of(j):
        return lax.rem(k + (j + experts), experts)

    def h_of(j):
        return lax.rem(h + (j + half), half)

    def remote(src, dst, send, recv, **where):
        return pltpu.make_async_remote_copy(
            src_ref=src, dst_ref=dst, send_sem=send, recv_sem=recv,
            device_id=where, device_id_type=pl.DeviceIdType.MESH,
        )

    def go(copy):
        copy.start()
        started.append(copy)

    weight_copies = (
        pltpu.make_async_copy(w_in_hbm.at[0], w_in, w_sem.at[0]),
        pltpu.make_async_copy(w_out_hbm.at[0], w_out, w_sem.at[1]),
    )
    barrier = pltpu.get_barrier_semaphore()
    for j in range(1, experts):
        pl.semaphore_signal(barrier, inc=1, device_id={"expert": z_of(j)}, device_id_type=pl.DeviceIdType.MESH)
    for i in range(1, mps):
        pl.semaphore_signal(barrier, inc=1, device_id={"mp": lax.rem(m + i, mps)}, device_id_type=pl.DeviceIdType.MESH)
    for copy in weight_copies:
        copy.start()

    def iota(shape, axis):
        return lax.broadcasted_iota(jnp.int32, shape, axis)

    def onehot(cond):
        return jnp.where(cond, 1.0, 0.0).astype(bf16)

    def below(row, bound):
        return jnp.sum((row < bound).astype(f32), axis=1, keepdims=True)

    def base_of(first, i):
        return jnp.floor((first + (chunks - 1 - i)) * (1.0 / chunks))

    def z_copy(u, j):
        return remote(zsend.at[u, j], zrecv.at[u, j], zs.at[u, j], zr.at[u, j], expert=z_of(j))

    cap = idx.shape[1]
    tok_col = iota((tok_dev, cap), 0) + k * tok_dev
    ones = jnp.ones((cap, most), bf16)
    lower = onehot(iota((tok_dev, tok_dev), 1) < iota((tok_dev, tok_dev), 0))
    rank_lane = iota((tok_dev, most), 1).astype(f32)
    far_first = sorted(range(1, experts), key=lambda j: -min(j, experts - j))
    near_first = far_first[::-1]

    def unit(i, a, f):
        return (i * 2 + a) * pieces + f

    def pack(i, a, f, j):
        u = unit(i, a, f)
        lo = f * width
        ref = dy if a else tok
        zsend[u, j] = mm(pt[i, j], ref[:, lo : lo + width], ROWS).astype(bf16)
        if j:
            go(z_copy(u, j))

    for n, j in enumerate(far_first + [0]):
        chosen = idx[pl.ds(z_of(j), 1), :]
        mark = mm(onehot(chosen == tok_col), ones)
        first = below(chosen, k * tok_dev)
        slot = mm(lower, mark.astype(bf16)) + first
        for i in range(chunks):
            pt[i, j] = onehot((slot == chunks * (base_of(first, i) + rank_lane) + i) & (mark > 0.5))
        if n == 0:
            pl.semaphore_wait(barrier, experts - 1 + mps - 1)
        pack(0, 0, 0, j)
    for i in range(chunks):
        for a in range(2):
            for f in range(pieces):
                if i + a + f:
                    for j in far_first + [0]:
                        pack(i, a, f, j)

    mine = idx[pl.ds(k, 1), :]
    slot_c, row_c = iota((slots, most), 0).astype(f32), iota((slots, most), 1).astype(f32)
    slot_t, row_t = iota((most, slots), 1).astype(f32), iota((most, slots), 0).astype(f32)
    for j in range(experts):
        for table, source, slot, row in ((cmat, z_of(-j), slot_c, row_c), (ctmat, z_of(j), slot_t, row_t)):
            first = below(mine, source * tok_dev)
            last = below(mine, (source + 1) * tok_dev)
            for i in range(chunks):
                table[i, j] = onehot((slot - row == base_of(first, i)) & (chunks * slot + i < last))

    def ag_slot(j, other):
        return h_of(-j) * 2 + ((1 - c) if other else c)

    def ag_across(u, j):
        return remote(full.at[u, 0], full.at[u, 2 * j], ags.at[u, j], agr.at[u, 2 * j], mp=h_of(j) * 2 + c)

    def ag_pair(u, j):
        return remote(full.at[u, 2 * j], full.at[u, 2 * j + 1], agf.at[u, j], agr.at[u, 2 * j + 1], mp=partner)

    def gather(i, a, f):
        u = unit(i, a, f)
        total = mm(cmat[i, 0], zsend[u, 0])
        for j in near_first:
            z_copy(u, j).wait_recv()
            total += mm(cmat[i, j], zrecv[u, j])
        full[u, 0] = total.astype(bf16)
        for j in range(1, half):
            go(ag_across(u, j))
        go(ag_pair(u, 0))

    def multiply(i, a, f, j, other, first):
        lo = pl.multiple_of(ag_slot(j, other) * columns + f * width, width)
        rows = full[unit(i, a, f), 2 * j + other]
        if a:
            term = mm(rows, w_out[:, pl.ds(lo, width)], COLS)
            acc = back
        else:
            term = mm(rows, w_in[pl.ds(lo, width), :])
            acc = pre
        if first:
            acc[i] = term
        else:
            acc[i] += term

    def use(i, a, f):
        u = unit(i, a, f)
        multiply(i, a, f, 0, 0, f == 0)
        for j in range(1, half):
            ag_across(u, j).wait_recv()
            go(ag_pair(u, j))
        ag_pair(u, 0).wait_recv()
        multiply(i, a, f, 0, 1, False)
        for j in range(1, half):
            multiply(i, a, f, j, 0, False)
        for j in range(1, half):
            ag_pair(u, j).wait_recv()
            multiply(i, a, f, j, 1, False)

    step = 32

    def gelu(i):
        def rows(n, carry):
            at = pl.ds(pl.multiple_of(n * step, step), step)
            v = pre[i, at, :]
            cumulative = 0.5 * (1.0 + lax.erf(v * inv_root_two))
            slopes[i, at, :] = cumulative + v * jnp.exp(-0.5 * v * v) * inv_root_tau
            pre[i, at, :] = v * cumulative
            return carry

        lax.fori_loop(0, slots // step, rows, 0)

    eye_slots = iota((slots, slots), 0) == iota((slots, slots), 1)

    def make_delta(i):
        def rows(n, carry):
            at = pl.ds(pl.multiple_of(n * step, step), step)
            g = back[i, at, :]
            delta[i, at, :] = (g * slopes[i, at, :]).astype(bf16)
            pre[i, at, 0:1] = jnp.sum(pre[i, at, :] * g, axis=1, keepdims=True)
            return carry

        lax.fori_loop(0, slots // step, rows, 0)
        gate_row = jnp.sum(jnp.where(eye_slots, pre[i, :, 0:1], 0.0), axis=0, keepdims=True)
        gmp[0, i] = jnp.broadcast_to(gate_row, (8, slots))

    def g_mp(n):
        return remote(gmp.at[0], gmp.at[n], gms.at[n], gmr.at[n], mp=lax.rem(m + n, mps))

    def g_z(j):
        return remote(gz.at[0], gz.at[j], gzs.at[j], gzr.at[j], expert=z_of(j))

    def contrib(i, f, j, other):
        lo = (h_of(j) * 2 + ((1 - c) if other else c)) * columns + f * width
        return mm(delta[i], w_in[pl.ds(pl.multiple_of(lo, width), width), :], COLS)

    def pair_sum(t, j):
        return remote(a_send.at[t, j], a_recv.at[t, j], as_.at[t, j], ar.at[t, j], mp=partner)

    def across_sum(t, j):
        return remote(b_send.at[t, j], b_recv.at[t, j], bs.at[t, j], br.at[t, j], mp=h_of(j) * 2 + c)

    order = list(range(1, half)) + [0]

    def scatter(i):
        for f in range(pieces):
            t = i * pieces + f
            for j in order:
                a_send[t, j] = contrib(i, f, j, 1).astype(bf16)
                go(pair_sum(t, j))
            for j in order:
                mine_sum = contrib(i, f, j, 0)
                pair_sum(t, j).wait_recv()
                mine_sum += a_recv[t, j].astype(f32)
                if j:
                    b_send[t, j] = mine_sum.astype(bf16)
                    go(across_sum(t, j))
                else:
                    own_sum[t] = mine_sum

    def back_copy(t, j):
        return remote(back_send.at[t, j], back_recv.at[t, j], xs.at[t, j], xr.at[t, j], expert=z_of(j))

    def send_back(i):
        for f in range(pieces):
            t = i * pieces + f
            total = own_sum[t]
            for j in range(1, half):
                across_sum(t, j).wait_recv()
                total += b_recv[t, j].astype(f32)
            rows = total.astype(bf16)
            for j in far_first + [0]:
                back_send[t, j] = mm(ctmat[i, j], rows).astype(bf16)
                if j:
                    go(back_copy(t, j))

    lanes = lgp.shape[1]
    eye_tok = iota((tok_dev, tok_dev), 0) == iota((tok_dev, tok_dev), 1)
    eye_most = iota((most, most), 0) == iota((most, most), 1)
    lane_e = iota((tok_dev, lanes), 1)
    slot_lane, rank_col = iota((most, slots), 1).astype(f32), iota((most, slots), 0).astype(f32)

    def gate_col(e):
        row = jax.nn.sigmoid(logits[pl.ds(e, 1), :])
        return jnp.sum(jnp.where(eye_tok, row, 0.0), axis=1, keepdims=True)

    def make_spread():
        for j in range(experts):
            gate = gate_col(z_of(j))
            for i in range(chunks):
                spread[i, j] = (pt[i, j].astype(f32) * gate).astype(bf16)

    def r_copy(j):
        return remote(rbuf.at[k], rbuf.at[k], rs.at[j], rr.at[j], expert=z_of(j))

    def r_arrival(j):
        return remote(rbuf.at[z_of(-j)], rbuf.at[z_of(-j)], rs.at[j], rr.at[j], expert=z_of(j))

    def router():
        lgp_val = jnp.zeros((tok_dev, lanes), f32)
        for j in range(experts):
            e = z_of(-j)
            if j:
                g_z(j).wait_recv()
            first = below(idx[pl.ds(e, 1), :], k * tok_dev)
            picked = jnp.zeros((tok_dev, 1), f32)
            for i in range(chunks):
                row = gz[j, i, 0:1, :]
                ranked = jnp.sum(jnp.where(slot_lane - rank_col == base_of(first, i), row, 0.0), axis=1, keepdims=True)
                ranked_row = jnp.sum(jnp.where(eye_most, ranked, 0.0), axis=0, keepdims=True)
                chosen = pt[i, (experts - j) % experts].astype(f32) > 0.5
                picked += jnp.sum(jnp.where(chosen, ranked_row, 0.0), axis=1, keepdims=True)
            gate = gate_col(e)
            lgp_val = jnp.where(lane_e == e, gate * (1.0 - gate) * picked, lgp_val)
        lgp[...] = lgp_val.astype(bf16)
        rwp[...] = jnp.zeros_like(rwp)
        rwp[0:experts, :] = router_w[...]
        local = mm(lgp[...], tok[...], ROWS)
        rbuf[k] = local[0 : rbuf.shape[1], :]
        for j in range(1, experts):
            go(r_copy(j))
        out[...] = mm(lgp[...], rwp[...])

    def gates():
        for n in range(1, mps):
            g_mp(n).wait_recv()
        for i in range(chunks):
            total = gmp[0, i]
            for n in range(1, mps):
                total += gmp[n, i]
            gz[0, i] = total
        for j in range(1, experts):
            go(g_z(j))

    for i in range(chunks):
        for f in range(pieces):
            gather(i, 0, f)
            if i == 0 and f == 0:
                weight_copies[0].wait()
        if i:
            send_back(i - 1)
        for f in range(pieces):
            if f == 0:
                for g in range(pieces):
                    if pieces > 1:
                        use(i, 0, g)
                if pieces > 1:
                    gelu(i)
            gather(i, 1, f)
            if i == 0 and f == 0:
                weight_copies[1].wait()
            if pieces == 1:
                use(i, 0, f)
                gelu(i)
            use(i, 1, f)
        make_delta(i)
        if i == chunks - 1:
            for n in range(1, mps):
                go(g_mp(n))
        scatter(i)
        if i == 0:
            make_spread()

    gates()
    send_back(chunks - 1)
    router()
    for i in range(chunks):
        for f in range(pieces):
            t = i * pieces + f
            lo = f * width
            total = out[:, lo : lo + width]
            for j in [0] + near_first:
                weights = spread[i, (experts - j) % experts]
                if j:
                    back_copy(t, j).wait_recv()
                    total += mm(weights, back_recv[t, j])
                else:
                    total += mm(weights, back_send[t, 0])
            out[:, lo : lo + width] = total

    for j in range(1, experts):
        r_arrival(j).wait_recv()
    summed = rbuf[0]
    for e in range(1, experts):
        summed += rbuf[e]
    router_out[...] = summed[0:experts, :]
    for copy in started:
        copy.wait_send()


def per_device(experts, mps, tokens_in, out_grad, logits, indices, w_in, w_out, router_w):
    tok_dev, columns = tokens_in.shape
    cap = indices.shape[1]
    most = min(tok_dev, 2 * cap // experts)
    chunks = CHUNKS if most % (16 * CHUNKS) == 0 else 1
    pieces = PIECES
    width = columns // pieces
    half = mps // 2
    slots = cap // chunks
    most = most // chunks
    features, hidden = w_in.shape[1:]
    rows8 = -(-experts // 8) * 8
    lanes = -(-experts // 128) * 128
    units, parts = 2 * chunks * pieces, chunks * pieces
    vmem = pl.BlockSpec(memory_space=pltpu.VMEM)
    hbm = pl.BlockSpec(memory_space=pl.ANY)
    dma = pltpu.SemaphoreType.DMA
    room = pltpu.VMEM
    input_grad, router_rows = pl.pallas_call(
        functools.partial(layer_kernel, experts, mps, chunks, pieces),
        out_shape=(
            jax.ShapeDtypeStruct((tok_dev, columns), f32),
            jax.ShapeDtypeStruct((experts, columns), f32),
        ),
        in_specs=[vmem, vmem, vmem, vmem, hbm, hbm, vmem],
        out_specs=(vmem, vmem),
        scratch_shapes=[
            room((features, hidden), bf16),
            room((hidden, features), bf16),
            room((chunks, experts, tok_dev, most), bf16),
            room((chunks, experts, tok_dev, most), bf16),
            room((chunks, experts, slots, most), bf16),
            room((chunks, experts, most, slots), bf16),
            room((units, experts, most, width), bf16),
            room((units, experts, most, width), bf16),
            room((units, mps, slots, width), bf16),
            room((chunks, slots, hidden), f32),
            room((chunks, slots, hidden), f32),
            room((chunks, slots, hidden), f32),
            room((chunks, slots, hidden), bf16),
            room((parts, half, slots, width), bf16),
            room((parts, half, slots, width), bf16),
            room((parts, half, slots, width), bf16),
            room((parts, half, slots, width), bf16),
            room((parts, slots, width), f32),
            room((parts, experts, most, width), bf16),
            room((parts, experts, most, width), bf16),
            room((mps, chunks, 8, slots), f32),
            room((experts, chunks, 8, slots), f32),
            room((experts, rows8, columns), f32),
            room((tok_dev, lanes), bf16),
            room((lanes, columns), bf16),
            dma((2,)),
            dma((units, experts)),
            dma((units, experts)),
            dma((units, half)),
            dma((units, half)),
            dma((units, mps)),
            dma((parts, half)),
            dma((parts, half)),
            dma((parts, half)),
            dma((parts, half)),
            dma((parts, experts)),
            dma((parts, experts)),
            dma((mps,)),
            dma((mps,)),
            dma((experts,)),
            dma((experts,)),
            dma((experts,)),
            dma((experts,)),
        ],
        compiler_params=pltpu.CompilerParams(collective_id=0, has_side_effects=True),
    )(tokens_in, out_grad, logits.T, indices, w_in, w_out, router_w.T)
    return input_grad, router_rows.T


def solution(mesh):
    return jax.shard_map(
        functools.partial(per_device, mesh.shape["expert"], mesh.shape["mp"]),
        mesh=mesh,
        in_specs=(
            P(("groups", "expert"), "mp"),
            P(("groups", "expert"), "mp"),
            P(("groups", "expert"), None),
            P("groups", None),
            P("expert", None, "mp"),
            P("expert", "mp", None),
            P("mp", None),
        ),
        out_specs=(P(("groups", "expert"), "mp"), P(("groups", "mp"), None)),
        check_vma=False,
    )
```

```python
import functools

import jax
import jax.numpy as jnp
from jax import lax
from jax.experimental import pallas as pl
from jax.experimental.pallas import tpu as pltpu
from jax.sharding import PartitionSpec as P

inv_root_two = 0.7071067811865476
inv_root_tau = 0.3989422804014327
bf16, f32 = jnp.bfloat16, jnp.float32
ROWS = ((0,), (0,))
COLS = ((1,), (1,))
CHUNKS = 2
PIECES = 2


def mm(a, b, dims=((1,), (0,))):
    return lax.dot_general(a, b, (dims, ((), ())), preferred_element_type=f32)


def layer_kernel(
    experts, mps, chunks, pieces,
    tok, dy, logits, idx, w_in_hbm, w_out_hbm, router_w,
    out, router_out,
    w_in, w_out, pt, spread, cmat, ctmat, zsend, zrecv, full, pre, back, slopes, delta,
    a_send, a_recv, b_send, b_recv, own_sum, back_send, back_recv,
    gmp, gz, rbuf, lgp, rwp,
    w_sem, zs, zr, ags, agf, agr, as_, ar, bs, br, xs, xr, gms, gmr, gzs, gzr, rs, rr,
):
    k = lax.axis_index("expert")
    m = lax.axis_index("mp")
    half = mps // 2
    h, c = lax.div(m, 2), lax.rem(m, 2)
    partner = h * 2 + (1 - c)
    tok_dev, columns = tok.shape
    slots = pre.shape[1]
    most = pt.shape[3]
    width = columns // pieces
    started = []

    def z_of(j):
        return lax.rem(k + (j + experts), experts)

    def h_of(j):
        return lax.rem(h + (j + half), half)

    def remote(src, dst, send, recv, **where):
        return pltpu.make_async_remote_copy(
            src_ref=src, dst_ref=dst, send_sem=send, recv_sem=recv,
            device_id=where, device_id_type=pl.DeviceIdType.MESH,
        )

    def go(copy):
        copy.start()
        started.append(copy)

    weight_copies = (
        pltpu.make_async_copy(w_in_hbm.at[0], w_in, w_sem.at[0]),
        pltpu.make_async_copy(w_out_hbm.at[0], w_out, w_sem.at[1]),
    )
    barrier = pltpu.get_barrier_semaphore()
    for j in range(1, experts):
        pl.semaphore_signal(barrier, inc=1, device_id={"expert": z_of(j)}, device_id_type=pl.DeviceIdType.MESH)
    for i in range(1, mps):
        pl.semaphore_signal(barrier, inc=1, device_id={"mp": lax.rem(m + i, mps)}, device_id_type=pl.DeviceIdType.MESH)
    for copy in weight_copies:
        copy.start()

    def iota(shape, axis):
        return lax.broadcasted_iota(jnp.int32, shape, axis)

    def onehot(cond):
        return jnp.where(cond, 1.0, 0.0).astype(bf16)

    def below(row, bound):
        return jnp.sum((row < bound).astype(f32), axis=1, keepdims=True)

    def base_of(first, i):
        return jnp.floor((first + (chunks - 1 - i)) * (1.0 / chunks))

    def z_copy(u, j):
        return remote(zsend.at[u, j], zrecv.at[u, j], zs.at[u, j], zr.at[u, j], expert=z_of(j))

    cap = idx.shape[1]
    tok_col = iota((tok_dev, cap), 0) + k * tok_dev
    ones = jnp.ones((cap, most), bf16)
    lower = onehot(iota((tok_dev, tok_dev), 1) < iota((tok_dev, tok_dev), 0))
    rank_lane = iota((tok_dev, most), 1).astype(f32)
    far_first = sorted(range(1, experts), key=lambda j: -min(j, experts - j))
    near_first = far_first[::-1]

    def unit(i, a, f):
        return (i * 2 + a) * pieces + f

    def pack(i, a, f, j):
        u = unit(i, a, f)
        lo = f * width
        ref = dy if a else tok
        zsend[u, j] = mm(pt[i, j], ref[:, lo : lo + width], ROWS).astype(bf16)
        if j:
            go(z_copy(u, j))

    for n, j in enumerate(far_first + [0]):
        chosen = idx[pl.ds(z_of(j), 1), :]
        mark = mm(onehot(chosen == tok_col), ones)
        first = below(chosen, k * tok_dev)
        slot = mm(lower, mark.astype(bf16)) + first
        for i in range(chunks):
            pt[i, j] = onehot((slot == chunks * (base_of(first, i) + rank_lane) + i) & (mark > 0.5))
        if n == 0:
            pl.semaphore_wait(barrier, experts - 1 + mps - 1)
        pack(0, 0, 0, j)
    for i in range(chunks):
        for a in range(2):
            for f in range(pieces):
                if i + a + f:
                    for j in far_first + [0]:
                        pack(i, a, f, j)

    mine = idx[pl.ds(k, 1), :]
    slot_c, row_c = iota((slots, most), 0).astype(f32), iota((slots, most), 1).astype(f32)
    slot_t, row_t = iota((most, slots), 1).astype(f32), iota((most, slots), 0).astype(f32)
    for j in range(experts):
        for table, source, slot, row in ((cmat, z_of(-j), slot_c, row_c), (ctmat, z_of(j), slot_t, row_t)):
            first = below(mine, source * tok_dev)
            last = below(mine, (source + 1) * tok_dev)
            for i in range(chunks):
                table[i, j] = onehot((slot - row == base_of(first, i)) & (chunks * slot + i < last))

    def ag_slot(j, other):
        return h_of(-j) * 2 + ((1 - c) if other else c)

    def ag_across(u, j):
        return remote(full.at[u, 0], full.at[u, 2 * j], ags.at[u, j], agr.at[u, 2 * j], mp=h_of(j) * 2 + c)

    def ag_pair(u, j):
        return remote(full.at[u, 2 * j], full.at[u, 2 * j + 1], agf.at[u, j], agr.at[u, 2 * j + 1], mp=partner)

    def gather(i, a, f):
        u = unit(i, a, f)
        total = mm(cmat[i, 0], zsend[u, 0])
        for j in near_first:
            z_copy(u, j).wait_recv()
            total += mm(cmat[i, j], zrecv[u, j])
        full[u, 0] = total.astype(bf16)
        for j in range(1, half):
            go(ag_across(u, j))
        go(ag_pair(u, 0))

    def multiply(i, a, f, j, other, first):
        lo = pl.multiple_of(ag_slot(j, other) * columns + f * width, width)
        rows = full[unit(i, a, f), 2 * j + other]
        if a:
            term = mm(rows, w_out[:, pl.ds(lo, width)], COLS)
            acc = back
        else:
            term = mm(rows, w_in[pl.ds(lo, width), :])
            acc = pre
        if first:
            acc[i] = term
        else:
            acc[i] += term

    def forward(i, a, f):
        u = unit(i, a, f)
        for j in range(1, half):
            ag_across(u, j).wait_recv()
            go(ag_pair(u, j))

    def use(i, a, f):
        u = unit(i, a, f)
        multiply(i, a, f, 0, 0, f == 0)
        ag_pair(u, 0).wait_recv()
        multiply(i, a, f, 0, 1, False)
        for j in range(1, half):
            multiply(i, a, f, j, 0, False)
        for j in range(1, half):
            ag_pair(u, j).wait_recv()
            multiply(i, a, f, j, 1, False)

    step = 32

    def gelu(i):
        def rows(n, carry):
            at = pl.ds(pl.multiple_of(n * step, step), step)
            v = pre[i, at, :]
            cumulative = 0.5 * (1.0 + lax.erf(v * inv_root_two))
            slopes[i, at, :] = cumulative + v * jnp.exp(-0.5 * v * v) * inv_root_tau
            pre[i, at, :] = v * cumulative
            return carry

        lax.fori_loop(0, slots // step, rows, 0)

    eye_slots = iota((slots, slots), 0) == iota((slots, slots), 1)

    def make_delta(i):
        def rows(n, carry):
            at = pl.ds(pl.multiple_of(n * step, step), step)
            g = back[i, at, :]
            delta[i, at, :] = (g * slopes[i, at, :]).astype(bf16)
            pre[i, at, 0:1] = jnp.sum(pre[i, at, :] * g, axis=1, keepdims=True)
            return carry

        lax.fori_loop(0, slots // step, rows, 0)
        gate_row = jnp.sum(jnp.where(eye_slots, pre[i, :, 0:1], 0.0), axis=0, keepdims=True)
        gmp[0, i] = jnp.broadcast_to(gate_row, (8, slots))

    def g_mp(n):
        return remote(gmp.at[0], gmp.at[n], gms.at[n], gmr.at[n], mp=lax.rem(m + n, mps))

    def g_z(j):
        return remote(gz.at[0], gz.at[j], gzs.at[j], gzr.at[j], expert=z_of(j))

    def contrib(i, f, j, other):
        lo = (h_of(j) * 2 + ((1 - c) if other else c)) * columns + f * width
        return mm(delta[i], w_in[pl.ds(pl.multiple_of(lo, width), width), :], COLS)

    def pair_sum(t, j):
        return remote(a_send.at[t, j], a_recv.at[t, j], as_.at[t, j], ar.at[t, j], mp=partner)

    def across_sum(t, j):
        return remote(b_send.at[t, j], b_recv.at[t, j], bs.at[t, j], br.at[t, j], mp=h_of(j) * 2 + c)

    order = list(range(1, half)) + [0]

    def scatter_pair(i):
        for f in range(pieces):
            t = i * pieces + f
            for j in order:
                a_send[t, j] = contrib(i, f, j, 1).astype(bf16)
                go(pair_sum(t, j))

    def scatter_across(i):
        for f in range(pieces):
            t = i * pieces + f
            for j in order:
                mine_sum = contrib(i, f, j, 0)
                pair_sum(t, j).wait_recv()
                mine_sum += a_recv[t, j].astype(f32)
                if j:
                    b_send[t, j] = mine_sum.astype(bf16)
                    go(across_sum(t, j))
                else:
                    own_sum[t] = mine_sum

    def back_copy(t, j):
        return remote(back_send.at[t, j], back_recv.at[t, j], xs.at[t, j], xr.at[t, j], expert=z_of(j))

    def send_back(i):
        for f in range(pieces):
            t = i * pieces + f
            total = own_sum[t]
            for j in range(1, half):
                across_sum(t, j).wait_recv()
                total += b_recv[t, j].astype(f32)
            rows = total.astype(bf16)
            for j in far_first + [0]:
                back_send[t, j] = mm(ctmat[i, j], rows).astype(bf16)
                if j:
                    go(back_copy(t, j))

    lanes = lgp.shape[1]
    eye_tok = iota((tok_dev, tok_dev), 0) == iota((tok_dev, tok_dev), 1)
    eye_most = iota((most, most), 0) == iota((most, most), 1)
    lane_e = iota((tok_dev, lanes), 1)
    slot_lane, rank_col = iota((most, slots), 1).astype(f32), iota((most, slots), 0).astype(f32)

    def gate_col(e):
        row = jax.nn.sigmoid(logits[pl.ds(e, 1), :])
        return jnp.sum(jnp.where(eye_tok, row, 0.0), axis=1, keepdims=True)

    def make_spread():
        for j in range(experts):
            gate = gate_col(z_of(j))
            for i in range(chunks):
                spread[i, j] = (pt[i, j].astype(f32) * gate).astype(bf16)

    def r_copy(j):
        return remote(rbuf.at[k], rbuf.at[k], rs.at[j], rr.at[j], expert=z_of(j))

    def r_arrival(j):
        return remote(rbuf.at[z_of(-j)], rbuf.at[z_of(-j)], rs.at[j], rr.at[j], expert=z_of(j))

    def router():
        lgp_val = jnp.zeros((tok_dev, lanes), f32)
        for j in range(experts):
            e = z_of(-j)
            if j:
                g_z(j).wait_recv()
            first = below(idx[pl.ds(e, 1), :], k * tok_dev)
            picked = jnp.zeros((tok_dev, 1), f32)
            for i in range(chunks):
                row = gz[j, i, 0:1, :]
                ranked = jnp.sum(jnp.where(slot_lane - rank_col == base_of(first, i), row, 0.0), axis=1, keepdims=True)
                ranked_row = jnp.sum(jnp.where(eye_most, ranked, 0.0), axis=0, keepdims=True)
                chosen = pt[i, (experts - j) % experts].astype(f32) > 0.5
                picked += jnp.sum(jnp.where(chosen, ranked_row, 0.0), axis=1, keepdims=True)
            gate = gate_col(e)
            lgp_val = jnp.where(lane_e == e, gate * (1.0 - gate) * picked, lgp_val)
        lgp[...] = lgp_val.astype(bf16)
        rwp[...] = jnp.zeros_like(rwp)
        rwp[0:experts, :] = router_w[...]
        local = mm(lgp[...], tok[...], ROWS)
        rbuf[k] = local[0 : rbuf.shape[1], :]
        for j in range(1, experts):
            go(r_copy(j))
        out[...] = mm(lgp[...], rwp[...])

    def gates():
        for n in range(1, mps):
            g_mp(n).wait_recv()
        for i in range(chunks):
            total = gmp[0, i]
            for n in range(1, mps):
                total += gmp[n, i]
            gz[0, i] = total
        for j in range(1, experts):
            go(g_z(j))

    pieces_of = range(pieces)
    for i in range(chunks + 1):
        now, past = i < chunks, i > 0
        if now:
            for f in pieces_of:
                gather(i, 0, f)
        if past:
            if i == 1:
                weight_copies[1].wait()
            for f in pieces_of:
                use(i - 1, 1, f)
            make_delta(i - 1)
            if not now:
                for n in range(1, mps):
                    go(g_mp(n))
            scatter_pair(i - 1)
        if now:
            for f in pieces_of:
                forward(i, 0, f)
            for f in pieces_of:
                gather(i, 1, f)
        if past:
            scatter_across(i - 1)
        if now:
            if i == 0:
                weight_copies[0].wait()
            for f in pieces_of:
                use(i, 0, f)
            for f in pieces_of:
                forward(i, 1, f)
            gelu(i)
            if i == 0:
                make_spread()
        else:
            gates()
        if past:
            send_back(i - 1)
    router()
    for i in range(chunks):
        for f in range(pieces):
            t = i * pieces + f
            lo = f * width
            total = out[:, lo : lo + width]
            for j in [0] + near_first:
                weights = spread[i, (experts - j) % experts]
                if j:
                    back_copy(t, j).wait_recv()
                    total += mm(weights, back_recv[t, j])
                else:
                    total += mm(weights, back_send[t, 0])
            out[:, lo : lo + width] = total

    for j in range(1, experts):
        r_arrival(j).wait_recv()
    summed = rbuf[0]
    for e in range(1, experts):
        summed += rbuf[e]
    router_out[...] = summed[0:experts, :]
    for copy in started:
        copy.wait_send()


def per_device(experts, mps, tokens_in, out_grad, logits, indices, w_in, w_out, router_w):
    tok_dev, columns = tokens_in.shape
    cap = indices.shape[1]
    most = min(tok_dev, 2 * cap // experts)
    chunks = CHUNKS if most % (16 * CHUNKS) == 0 else 1
    pieces = PIECES
    width = columns // pieces
    half = mps // 2
    slots = cap // chunks
    most = most // chunks
    features, hidden = w_in.shape[1:]
    rows8 = -(-experts // 8) * 8
    lanes = -(-experts // 128) * 128
    units, parts = 2 * chunks * pieces, chunks * pieces
    vmem = pl.BlockSpec(memory_space=pltpu.VMEM)
    hbm = pl.BlockSpec(memory_space=pl.ANY)
    dma = pltpu.SemaphoreType.DMA
    room = pltpu.VMEM
    input_grad, router_rows = pl.pallas_call(
        functools.partial(layer_kernel, experts, mps, chunks, pieces),
        out_shape=(
            jax.ShapeDtypeStruct((tok_dev, columns), f32),
            jax.ShapeDtypeStruct((experts, columns), f32),
        ),
        in_specs=[vmem, vmem, vmem, vmem, hbm, hbm, vmem],
        out_specs=(vmem, vmem),
        scratch_shapes=[
            room((features, hidden), bf16),
            room((hidden, features), bf16),
            room((chunks, experts, tok_dev, most), bf16),
            room((chunks, experts, tok_dev, most), bf16),
            room((chunks, experts, slots, most), bf16),
            room((chunks, experts, most, slots), bf16),
            room((units, experts, most, width), bf16),
            room((units, experts, most, width), bf16),
            room((units, mps, slots, width), bf16),
            room((chunks, slots, hidden), f32),
            room((chunks, slots, hidden), f32),
            room((chunks, slots, hidden), f32),
            room((chunks, slots, hidden), bf16),
            room((parts, half, slots, width), bf16),
            room((parts, half, slots, width), bf16),
            room((parts, half, slots, width), bf16),
            room((parts, half, slots, width), bf16),
            room((parts, slots, width), f32),
            room((parts, experts, most, width), bf16),
            room((parts, experts, most, width), bf16),
            room((mps, chunks, 8, slots), f32),
            room((experts, chunks, 8, slots), f32),
            room((experts, rows8, columns), f32),
            room((tok_dev, lanes), bf16),
            room((lanes, columns), bf16),
            dma((2,)),
            dma((units, experts)),
            dma((units, experts)),
            dma((units, half)),
            dma((units, half)),
            dma((units, mps)),
            dma((parts, half)),
            dma((parts, half)),
            dma((parts, half)),
            dma((parts, half)),
            dma((parts, experts)),
            dma((parts, experts)),
            dma((mps,)),
            dma((mps,)),
            dma((experts,)),
            dma((experts,)),
            dma((experts,)),
            dma((experts,)),
        ],
        compiler_params=pltpu.CompilerParams(collective_id=0, has_side_effects=True),
    )(tokens_in, out_grad, logits.T, indices, w_in, w_out, router_w.T)
    return input_grad, router_rows.T


def solution(mesh):
    return jax.shard_map(
        functools.partial(per_device, mesh.shape["expert"], mesh.shape["mp"]),
        mesh=mesh,
        in_specs=(
            P(("groups", "expert"), "mp"),
            P(("groups", "expert"), "mp"),
            P(("groups", "expert"), None),
            P("groups", None),
            P("expert", None, "mp"),
            P("expert", "mp", None),
            P("mp", None),
        ),
        out_specs=(P(("groups", "expert"), "mp"), P(("groups", "mp"), None)),
        check_vma=False,
    )
```
